512 devices in a mesh: ctx: 32 (over x, z_lo, core), head: 16 (over y, z_hi).
Axes of the slice: x: 4, y: 8, z: 8 (z_hi: 2, z_lo: 4; z = z_hi * 4 + z_lo), core: 2. Of those that a mesh axis runs over, the one named last changes fastest.
Arguments:
- queries: bfloat16 [4096, 8192], P('ctx', 'head'), may hold values from -9 to 9
- keys: bfloat16 [4096, 8192], P('ctx', 'head'), may hold values from -6 to 6
- values: bfloat16 [4096, 8192], P('ctx', 'head'), may hold values from -6 to 6
- d_out: bfloat16 [4096, 8192], P(('ctx', 'head')), may hold values from -6 to 6
- block_lists: int32 [32, 8], replicated, may hold values from 0 to 31, as said below
- list_counts: int32 [32], replicated, may hold values from 1 to 8, as said below
Outputs:
- attn_out: bfloat16 [4096, 8192], P('ctx', 'head')
- grad_q: bfloat16 [4096, 8192], P('ctx', 'head')
- grad_k: bfloat16 [4096, 8192], P('ctx', 'head')
- grad_v: bfloat16 [4096, 8192], P('ctx', 'head')
The draws below stay inside these ranges and needn't reach their ends.
Inputs may be any that keep to these rules, and one draw needn't show every extreme that they name: `block_lists`: each row holds 8 distinct patch block ids; only the first list_counts entries of a row are read. Patch block p is held by index p of ctx. `list_counts`: some text block reads 8 patch blocks.
All inputs are finite; a program needn't handle non-finite values.
Results may differ from the reference program's by a relative error of at most 0.022.
Values may be sent and summed in bfloat16 or wider, within the bound.
A program may use at most 64 MiB of HBM per device.

```python
import math
import jax
import jax.numpy as jnp
from jax import lax

DH = 128
BLK = 128
MAXB = 8
HEADS = 64
QBLK = 32
PBLK = 32
TEXT = 4096
PATCH = 4096


def list_draw(key):
    base = jax.random.fold_in(key, 101)
    key_pop, key_score, key_count, key_full = jax.random.split(base, 4)
    popularity = jax.random.randint(key_pop, (PBLK,), 0, 3 * PBLK)
    noise = jax.random.randint(key_score, (QBLK, PBLK), 0, 3 * PBLK)
    ranked = (noise + popularity[None, :]) * PBLK + jnp.arange(PBLK, dtype=jnp.int32)[None, :]
    chosen = lax.top_k(ranked, MAXB)[1].astype(jnp.int32)
    counts = jax.random.randint(key_count, (QBLK,), 1, MAXB + 1)
    full_at = jax.random.randint(key_full, (), 0, QBLK)
    counts = counts.at[full_at].set(MAXB)
    return (chosen, counts.astype(jnp.int32))


def key_field(key):
    raw = jnp.clip(jax.random.normal(jax.random.fold_in(key, 202), (PATCH, HEADS * DH), jnp.float32), -6.0, 6.0)
    return raw


def draw_block_lists(key, part):
    return list_draw(key)[0]


def draw_list_counts(key, part):
    return list_draw(key)[1]


def draw_keys(key, part):
    return key_field(key).astype(jnp.bfloat16)


def draw_queries(key, part):
    raw = jnp.clip(jax.random.normal(jax.random.fold_in(key, 404), (TEXT, HEADS * DH), jnp.float32), -6.0, 6.0)
    return raw.astype(jnp.bfloat16)


def block_scale(rng, shape, cuts, low, largest):
    factor_of, own = 1.0, jax.random.fold_in(rng, 6)
    for position, parts in cuts:
        draws = jnp.exp(jax.random.uniform(jax.random.fold_in(own, position), (parts,), jnp.float32, low / len(cuts), largest / len(cuts)))
        factor_of = factor_of * jnp.repeat(draws, shape[position] // parts).reshape([-1 if axis == position else 1 for axis in range(len(shape))])
    return factor_of


def gaussian(stream_key, dims, scale, bound, cuts=(), kind=jnp.bfloat16):
    entries = scale * jax.random.normal(stream_key, dims, jnp.float32)
    if cuts:
        entries = entries * block_scale(stream_key, dims, cuts, -0.22, 0.18)
    return jnp.clip(entries, -bound, bound).astype(kind)


def setup_inputs(seed: int = 0) -> dict:
    seeds = jax.random.split(jax.random.key(seed), 7)
    return {
        "queries": draw_queries(jax.random.fold_in(seeds[6], 71), 0),
        "keys": draw_keys(jax.random.fold_in(seeds[6], 71), 0),
        "values": gaussian(seeds[2], (PATCH, HEADS * DH), 1.0, 6.0, ((0, 32), (1, 16))),
        "d_out": gaussian(seeds[3], (TEXT, HEADS * DH), 1.0, 6.0, ((0, 512),)),
        "block_lists": draw_block_lists(jax.random.fold_in(seeds[6], 71), 0),
        "list_counts": draw_list_counts(jax.random.fold_in(seeds[6], 71), 0),
    }


def reference(queries, keys, values, d_out, block_lists, list_counts):
    heads = queries.shape[1] // DH
    scale = 1.0 / math.sqrt(DH)
    text_blocks = queries.shape[0] // BLK
    keys_full = keys.astype(jnp.float32).reshape(-1, heads, DH)
    values_full = values.astype(jnp.float32).reshape(-1, heads, DH)
    q_blocks = queries.reshape(text_blocks, BLK, heads, DH)
    d_blocks = d_out.reshape(text_blocks, BLK, heads, DH)
    key_block = jnp.arange(keys.shape[0], dtype=jnp.int32) // BLK
    slot_ids = jnp.arange(block_lists.shape[1], dtype=jnp.int32)

    def step(carry, inputs):
        grad_keys, grad_values = carry
        q_block, d_block, list_row, list_count = inputs
        live = slot_ids < list_count
        mask = jnp.any((list_row[:, None] == key_block[None, :]) & live[:, None], axis=0)
        q_float = q_block.astype(jnp.float32)
        d_float = d_block.astype(jnp.float32)
        scores = jnp.einsum('qhd,khd->hqk', q_float, keys_full) * scale
        masked = jnp.where(mask[None, None, :], scores, -jnp.inf)
        row_max = lax.optimization_barrier(jnp.max(masked, axis=-1))
        row_total = lax.optimization_barrier(jnp.sum(jnp.exp(masked - row_max[..., None]), axis=-1))
        log_total = row_max + jnp.log(row_total)
        probs = jnp.exp(masked - log_total[..., None])
        weights = probs.astype(jnp.bfloat16)
        attn_block = jnp.einsum('hqk,khd->qhd', weights.astype(jnp.float32), values_full).astype(jnp.bfloat16)
        row_delta = lax.optimization_barrier(jnp.sum(attn_block.astype(jnp.float32) * d_float, axis=-1)).T
        dprobs = jnp.einsum('qhd,khd->hqk', d_float, values_full)
        dscores = (probs * (dprobs - row_delta[..., None])).astype(jnp.bfloat16)
        grad_block = (jnp.einsum('hqk,khd->qhd', dscores.astype(jnp.float32), keys_full) * scale).astype(jnp.bfloat16)
        grad_keys = grad_keys + jnp.einsum('hqk,qhd->khd', dscores.astype(jnp.float32), q_float)
        grad_values = grad_values + jnp.einsum('hqk,qhd->khd', weights.astype(jnp.float32), d_float)
        return ((grad_keys, grad_values), (attn_block, grad_block))
    start = (jnp.zeros(keys_full.shape, jnp.float32), jnp.zeros(keys_full.shape, jnp.float32))
    (grad_keys, grad_values), (attn_blocks, grad_blocks) = lax.scan(step, start, (q_blocks, d_blocks, block_lists, list_counts))
    attn_out = attn_blocks.reshape(queries.shape)
    grad_q = grad_blocks.reshape(queries.shape)
    grad_k = (grad_keys * scale).astype(jnp.bfloat16).reshape(keys.shape)
    grad_v = grad_values.astype(jnp.bfloat16).reshape(values.shape)
    return (attn_out, grad_q, grad_k, grad_v)
```

```python
import functools
import math

import jax
import jax.numpy as jnp
from jax import lax
from jax.experimental import pallas as pl
from jax.experimental.pallas import tpu as pltpu
from jax.sharding import PartitionSpec as P

DH = 128
BLK = 128
MAXB = 8
NX, NZ, NC = 4, 4, 2
NPOS = NX * NZ * NC
GROUP = 4
MESH = pl.DeviceIdType.MESH
BF16, F32 = jnp.bfloat16, jnp.float32
SCALE = 1.0 / math.sqrt(DH)
LOG2E = math.log2(math.e)


def coords():
    i = lax.axis_index("ctx")
    return i // (NZ * NC), (i // NC) % NZ, i % NC


def ctx_id(x, z, c):
    return {"ctx": x * (NZ * NC) + z * NC + c}


def slot_of(x, z, c):
    return c * (NX * NZ) + x * NZ + z


def send(src, dst, send_sem, recv_sem, device):
    copy = pltpu.make_async_remote_copy(
        src_ref=src, dst_ref=dst, send_sem=send_sem, recv_sem=recv_sem,
        device_id=device, device_id_type=MESH,
    )
    copy.start()
    return copy


def enter(partners):
    barrier = pltpu.get_barrier_semaphore()
    for partner in partners:
        pl.semaphore_signal(barrier, inc=1, device_id=partner, device_id_type=MESH)
    pl.semaphore_wait(barrier, len(partners))


def gather_kernel(
    heads, q, k, v, d, kh, vh, qh, dh, d_rows,
    z_send, z_recv, x_send, x_recv, c_send, c_recv, h_send, h_recv, local,
):
    x, z, c = coords()
    g = lax.axis_index("head")
    right, left = (x + 1) % NX, (x + 3) % NX
    to_right, to_left = ctx_id(right, z, c), ctx_id(left, z, c)
    sibling = ctx_id(x, z, 1 - c)
    z_of = [(z + r) % NZ for r in range(NZ)]
    enter(
        [ctx_id(x, z_of[r], c) for r in range(1, NZ)]
        + [to_right, to_left, sibling]
        + [{"head": (g + r) % heads} for r in range(1, heads)]
    )
    mine = slot_of(x, z, c)
    copies = []

    def columns(ref, head):
        return ref.at[:, pl.ds(pl.multiple_of(head * DH, DH), DH)]

    def spread(index, ref, dst):
        got = []
        for r in range(1, NZ):
            copies.append(send(
                columns(ref, z_of[r]), dst, z_send.at[index, r], z_recv.at[index, r],
                ctx_id(x, z_of[r], c),
            ))
            got.append(copies[-1])
        own = pltpu.make_async_copy(columns(ref, z), dst, local.at[index])
        own.start()
        return got, own

    def settle(parts):
        got, own = parts
        own.wait()
        for copy in got:
            copy.wait_recv()

    k_parts = spread(0, k, kh.at[mine])
    v_parts = spread(1, v, vh.at[mine])
    d_parts = []
    for r in range(1, heads):
        there = (g + r) % heads
        d_parts.append(send(
            d.at[:, pl.ds(pl.multiple_of(there * (GROUP * DH), GROUP * DH), GROUP * DH)],
            d_rows.at[g], h_send.at[r], h_recv.at[r], {"head": there},
        ))
    d_own = pltpu.make_async_copy(
        d.at[:, pl.ds(pl.multiple_of(g * (GROUP * DH), GROUP * DH), GROUP * DH)],
        d_rows.at[g], local.at[4],
    )
    d_own.start()
    copies.extend(d_parts)
    q_parts = spread(2, q, qh.at[z])

    def shard(ref, chip, core):
        return ref.at[pl.ds(core * (NX * NZ) + chip * NZ, NZ)]

    def pass_on(index, ref, chip, device, sems, slot):
        part = shard(ref, chip, c)
        copies.append(send(
            part, part, sems[0].at[index, slot], sems[1].at[index, slot], device,
        ))
        return copies[-1]

    x_sems, c_sems = (x_send, x_recv), (c_send, c_recv)
    settle(k_parts)
    k_right = pass_on(0, kh, x, to_right, x_sems, 0)
    k_left = pass_on(0, kh, x, to_left, x_sems, 1)
    sib = [pass_on(0, kh, x, sibling, c_sems, 0)]
    settle(v_parts)
    v_left = pass_on(1, vh, x, to_left, x_sems, 1)
    v_right = pass_on(1, vh, x, to_right, x_sems, 0)
    sib.append(pass_on(1, vh, x, sibling, c_sems, 0))
    k_right.wait_recv()
    k_far = pass_on(0, kh, left, to_right, x_sems, 2)
    sib.append(pass_on(0, kh, left, sibling, c_sems, 1))
    v_left.wait_recv()
    v_far = pass_on(1, vh, right, to_left, x_sems, 2)
    sib.append(pass_on(1, vh, right, sibling, c_sems, 1))
    k_left.wait_recv()
    sib.append(pass_on(0, kh, right, sibling, c_sems, 2))
    v_right.wait_recv()
    sib.append(pass_on(1, vh, left, sibling, c_sems, 2))
    d_own.wait()
    for copy in d_parts:
        copy.wait_recv()
    dz = []
    for r in range(1, NZ):
        head = pl.multiple_of(z_of[r] * DH, DH)
        copies.append(send(
            d_rows.at[:, :, pl.ds(head, DH)], dh.at[z], z_send.at[3, r], z_recv.at[3, r],
            ctx_id(x, z_of[r], c),
        ))
        dz.append(copies[-1])
    dz_own = pltpu.make_async_copy(
        d_rows.at[:, :, pl.ds(pl.multiple_of(z * DH, DH), DH)], dh.at[z], local.at[3]
    )
    dz_own.start()
    far = (x + 2) % NX
    k_far.wait_recv()
    sib.append(pass_on(0, kh, far, sibling, c_sems, 3))
    v_far.wait_recv()
    sib.append(pass_on(1, vh, far, sibling, c_sems, 3))
    settle(q_parts)
    settle((dz, dz_own))
    for copy in sib:
        copy.wait_recv()
    for copy in copies:
        copy.wait_send()


def attend_kernel(
    lists, counts, q, k, v, d, attn, grad_q, grad_k, grad_v, k_acc, v_acc, k_rows, v_rows
):
    x, z, c = coords()
    k_acc[...] = jnp.zeros_like(k_acc)
    v_acc[...] = jnp.zeros_like(v_acc)
    contract_last = (((1,), (1,)), ((), ()))
    contract_first = (((0,), (0,)), ((), ()))

    def text_block(b, _):
        t = x * (NZ * NC) + b * NC + c
        count = counts[t]
        slots = []
        for j in range(MAXB):
            p = lists[t, j]
            slot = slot_of(p // (NZ * NC), (p // NC) % NZ, p % NC)
            slots.append(slot)
            k_rows[pl.ds(j * BLK, BLK), :] = k[slot]
            v_rows[pl.ds(j * BLK, BLK), :] = v[slot]
        qb, db = q[b], d[b]
        keys, vals = k_rows[...], v_rows[...]
        scores = lax.dot_general(keys, qb, contract_last, preferred_element_type=F32)
        live = lax.broadcasted_iota(jnp.int32, scores.shape, 0) < count * BLK
        scores = jnp.where(live, scores, -jnp.inf)
        top = jnp.max(scores, axis=0, keepdims=True)
        e = jnp.exp2((scores - top) * (SCALE * LOG2E))
        total = jnp.sum(e, axis=0, keepdims=True)
        probs = e * (1.0 / total)
        weights = probs.astype(BF16)
        dprobs = lax.dot_general(vals, db, contract_last, preferred_element_type=F32)
        delta = jnp.sum(weights.astype(F32) * dprobs, axis=0, keepdims=True)
        dscores = (probs * (dprobs - delta)).astype(BF16)
        attn[b] = lax.dot_general(
            weights, vals, contract_first, preferred_element_type=F32
        ).astype(BF16)
        grad_q[b] = (
            lax.dot_general(dscores, keys, contract_first, preferred_element_type=F32) * SCALE
        ).astype(BF16)
        dv = jnp.dot(weights, db, preferred_element_type=F32)
        dk = jnp.dot(dscores, qb, preferred_element_type=F32)
        for j in range(MAXB):
            v_acc[slots[j]] += dv[j * BLK : (j + 1) * BLK]
            k_acc[slots[j]] += dk[j * BLK : (j + 1) * BLK]
        return 0

    lax.fori_loop(0, NZ, text_block, 0)
    grad_k[...] = (k_acc[...] * SCALE).astype(BF16)
    grad_v[...] = v_acc[...].astype(BF16)


def scatter_kernel(
    attn_in, gq_in, dk_in, dv_in, attn, grad_q, grad_k, grad_v,
    sib_in, sums, x_in, final,
    z_send, z_recv, x_send, x_recv, c_send, c_recv, local,
):
    x, z, c = coords()
    right, left, far = (x + 1) % NX, (x + 3) % NX, (x + 2) % NX
    to_right, to_left = ctx_id(right, z, c), ctx_id(left, z, c)
    sibling = ctx_id(x, z, 1 - c)
    z_of = [(z + r) % NZ for r in range(NZ)]
    enter([ctx_id(x, z_of[r], c) for r in range(1, NZ)] + [to_right, to_left, sibling])
    copies = []

    def columns(ref):
        return ref.at[:, pl.ds(pl.multiple_of(z * DH, DH), DH)]

    def spread(index, ref, out):
        got = []
        for r in range(1, NZ):
            copies.append(send(
                ref.at[z_of[r]], columns(out), z_send.at[index, r], z_recv.at[index, r],
                ctx_id(x, z_of[r], c),
            ))
            got.append(copies[-1])
        own = pltpu.make_async_copy(ref.at[z], columns(out), local.at[index])
        own.start()
        return got, own

    partial = (dk_in, dv_in)
    order = ((far, left, right, x), (far, right, left, x))
    sib = [[None] * NX, [None] * NX]
    for n in range(NX):
        for i in range(2):
            chip = order[i][n]
            sib[i][n] = send(
                partial[i].at[pl.ds((1 - c) * (NX * NZ) + chip * NZ, NZ)],
                sib_in.at[i, n], c_send.at[i, n], c_recv.at[i, n], sibling,
            )
            copies.append(sib[i][n])
    parts = [spread(0, attn_in, attn), spread(1, gq_in, grad_q)]
    forward, back = (to_right, to_left), (to_left, to_right)

    def add(i, n, others, out):
        sib[i][n].wait_recv()
        base = c * (NX * NZ) + order[i][n] * NZ

        def block(j, _):
            total = partial[i][base + j].astype(F32) + sib_in[i, n, j].astype(F32)
            for other in others:
                total = total + x_in[i, other, j].astype(F32)
            out[j] = total.astype(BF16)
            return 0

        lax.fori_loop(0, NZ, block, 0)

    def ship(i, n, device):
        copies.append(send(
            sums.at[i, n], x_in.at[i, n], x_send.at[i, n], x_recv.at[i, n], device
        ))
        return copies[-1]

    moves = [[], []]
    for i in range(2):
        add(i, 0, (), sums.at[i, 0])
        moves[i].append(ship(i, 0, forward[i]))
    for i in range(2):
        add(i, 1, (), sums.at[i, 1])
        moves[i].append(ship(i, 1, back[i]))
    for i in range(2):
        moves[i][0].wait_recv()
        add(i, 2, (0,), sums.at[i, 2])
        moves[i].append(ship(i, 2, forward[i]))
    for i in range(2):
        moves[i][1].wait_recv()
        moves[i][2].wait_recv()
        add(i, 3, (1, 2), final.at[i])
        parts.append(spread(2 + i, final.at[i], (grad_k, grad_v)[i]))
    for got, own in parts:
        own.wait()
        for copy in got:
            copy.wait_recv()
    for copy in copies:
        copy.wait_send()


def shards(queries, keys, values, d_out, block_lists, list_counts):
    heads = lax.axis_size("head")
    hbm = pl.BlockSpec(memory_space=pl.ANY)
    vmem = pl.BlockSpec(memory_space=pltpu.VMEM)
    smem = pl.BlockSpec(memory_space=pltpu.SMEM)
    dma = pltpu.SemaphoreType.DMA
    blocks = jax.ShapeDtypeStruct((NPOS, BLK, DH), BF16)
    mine = jax.ShapeDtypeStruct((NZ, BLK, DH), BF16)
    rows = BLK // heads
    kh, vh, qh, dh, _ = pl.pallas_call(
        functools.partial(gather_kernel, heads),
        out_shape=(
            blocks, blocks, mine,
            jax.ShapeDtypeStruct((NZ, heads, rows, DH), BF16),
            jax.ShapeDtypeStruct((heads, rows, GROUP * DH), BF16),
        ),
        in_specs=[hbm] * 4,
        out_specs=[hbm] * 5,
        scratch_shapes=[
            dma((4, NZ)), dma((4, NZ)), dma((2, 3)), dma((2, 3)), dma((2, NX)), dma((2, NX)),
            dma((heads,)), dma((heads,)), dma((5,)),
        ],
        compiler_params=pltpu.CompilerParams(collective_id=0, has_side_effects=True),
        name="gather",
    )(queries, keys, values, d_out)
    attn_b, gq_b, dk_b, dv_b = pl.pallas_call(
        attend_kernel,
        out_shape=(mine, mine, blocks, blocks),
        in_specs=[smem, smem] + [vmem] * 4,
        out_specs=[vmem] * 4,
        scratch_shapes=[
            pltpu.VMEM((NPOS, BLK, DH), F32), pltpu.VMEM((NPOS, BLK, DH), F32),
            pltpu.VMEM((MAXB * BLK, DH), BF16), pltpu.VMEM((MAXB * BLK, DH), BF16),
        ],
        compiler_params=pltpu.CompilerParams(vmem_limit_bytes=48 << 20),
        name="attend",
    )(block_lists, list_counts, qh, kh, vh, dh.reshape(NZ, BLK, DH))
    out = jax.ShapeDtypeStruct((BLK, GROUP * DH), BF16)
    return pl.pallas_call(
        scatter_kernel,
        out_shape=(out,) * 4,
        in_specs=[vmem] * 4,
        out_specs=[hbm] * 4,
        scratch_shapes=[
            pltpu.VMEM((2, NX, NZ, BLK, DH), BF16),
            pltpu.VMEM((2, 3, NZ, BLK, DH), BF16),
            pltpu.VMEM((2, 3, NZ, BLK, DH), BF16),
            pltpu.VMEM((2, NZ, BLK, DH), BF16),
            dma((4, NZ)), dma((4, NZ)), dma((2, 3)), dma((2, 3)), dma((2, NX)), dma((2, NX)),
            dma((4,)),
        ],
        compiler_params=pltpu.CompilerParams(
            collective_id=1, has_side_effects=True, vmem_limit_bytes=48 << 20
        ),
        name="scatter",
    )(attn_b, gq_b, dk_b, dv_b)


def solution(mesh):
    spec = P("ctx", "head")
    return jax.shard_map(
        shards,
        mesh=mesh,
        in_specs=(spec, spec, spec, P(("ctx", "head"), None), P(), P()),
        out_specs=(spec,) * 4,
        check_vma=False,
    )
```

```python
import math

import jax
import jax.numpy as jnp
from jax import lax
from jax.experimental import pallas as pl
from jax.experimental.pallas import tpu as pltpu
from jax.sharding import PartitionSpec as P

DH = 128
BLK = 128
MAXB = 8
NX, NY, NZ, NC = 4, 8, 4, 2
NPOS = NX * NZ * NC
GROUP = 4
MESH = pl.DeviceIdType.MESH
BF16, F32 = jnp.bfloat16, jnp.float32
SCALE = 1.0 / math.sqrt(DH)
LOG2E = math.log2(math.e)
LAST = (((1,), (1,)), ((), ()))
FIRST = (((0,), (0,)), ((), ()))


def coords():
    i = lax.axis_index("ctx")
    return i // (NZ * NC), (i // NC) % NZ, i % NC


def head_coords():
    g = lax.axis_index("head")
    return g // 2, g % 2


def z_order(z):
    return [z, z + 1 - 2 * (z % 2), (z + 2) % NZ, NZ - 1 - z]


def ctx_id(x, z, c):
    return {"ctx": x * (NZ * NC) + z * NC + c}


def slot_of(x, z, c):
    return c * (NX * NZ) + x * NZ + z


def send(src, dst, send_sem, recv_sem, device):
    copy = pltpu.make_async_remote_copy(
        src_ref=src, dst_ref=dst, send_sem=send_sem, recv_sem=recv_sem,
        device_id=device, device_id_type=MESH,
    )
    copy.start()
    return copy


def columns(ref, start, width):
    return ref.at[:, pl.ds(pl.multiple_of(start, DH), width)]


def kernel(
    lists, counts, q, k, v, d, attn, grad_q, grad_k, grad_v,
    kh, vh, qh, dh, d_rows, where, k_rows, v_rows, probs, weights, dscores, d_cat, own_out,
    lhs, give, sib_in, sums, x_in, final,
    z_send, z_recv, x_send, x_recv, c_send, c_recv, y_send, y_recv, d_send, d_recv,
    oz_send, oz_recv, ox_send, ox_recv, oc_send, oc_recv, local,
):
    x, z, c = coords()
    y, h = head_coords()
    right, left, far = (x + 1) % NX, (x + 3) % NX, (x + 2) % NX
    to_right, to_left, sibling = ctx_id(right, z, c), ctx_id(left, z, c), ctx_id(x, z, 1 - c)
    z_of = z_order(z)

    def z_id(n, flip):
        return {**ctx_id(x, z_of[n], c), "head": 2 * y + (h if flip == 0 else 1 - h)}

    def y_id(r):
        return {"head": 2 * ((y + r) % NY) + h}

    partners = (
        [ctx_id(x, z_of[n], c) for n in range(1, NZ)]
        + [to_right, to_left, sibling]
        + [y_id(r) for r in range(1, NY)]
        + [z_id(n, 1) for n in range(NZ)]
    )
    barrier = pltpu.get_barrier_semaphore()
    for partner in partners:
        pl.semaphore_signal(barrier, inc=1, device_id=partner, device_id_type=MESH)
    pl.semaphore_wait(barrier, len(partners))
    copies = []

    def go(*args):
        copies.append(send(*args))
        return copies[-1]

    def keep(src, dst, sem):
        copy = pltpu.make_async_copy(src, dst, sem)
        copy.start()
        return copy

    ins, outs = (k, v, q), (kh, vh, qh)

    def across(i, n):
        place = slot_of(x, z, c) if i < 2 else z
        return go(
            columns(ins[i], z_of[n] * DH, DH), outs[i].at[place],
            z_send.at[i, n], z_recv.at[i, n], ctx_id(x, z_of[n], c),
        )

    def along(i, n, role):
        to = (to_right, to_left, (to_right, to_left)[i])[role]
        chip = (x, x, (left, right)[i])[role]
        dst = outs[i].at[slot_of(chip, z_of[n], c)]
        src = columns(ins[i], z * DH, DH) if role < 2 and n == 0 else dst
        return go(src, dst, x_send.at[i, role, n], x_recv.at[i, role, n], to)

    def over(i, m, chip):
        part = outs[i].at[pl.ds(c * (NX * NZ) + chip * NZ, NZ)]
        return go(part, part, c_send.at[i, m], c_recv.at[i, m], sibling)

    zs = [[None] * NZ for _ in range(3)]
    xs = [[[None] * NZ for _ in range(3)] for _ in range(2)]
    sib = [[], []]

    def own_block(i, n):
        if n > 0:
            zs[i][n].wait_recv()
        for role in range(2):
            xs[i][role][n] = along(i, n, role)

    def pass_on(i, n):
        xs[i][i][n].wait_recv()
        xs[i][2][n] = along(i, n, 2)

    def rest(i):
        other = 1 - i
        for n in range(NZ):
            xs[i][other][n].wait_recv()
        sib[i].append(over(i, 2, (right, left)[i]))
        for n in range(NZ):
            xs[i][2][n].wait_recv()
        sib[i].append(over(i, 3, far))

    for i in range(2):
        for n in range(1, NZ):
            zs[i][n] = across(i, n)
        own_block(i, 0)
    own = [
        keep(columns(ins[i], z * DH, DH), outs[i].at[slot_of(x, z, c) if i < 2 else z], local.at[i])
        for i in range(3)
    ]
    ys = [
        go(
            columns(d, ((y + r) % NY) * (2 * GROUP * DH), 2 * GROUP * DH), d_rows.at[y],
            y_send.at[r], y_recv.at[r], y_id(r),
        )
        for r in range(1, NY)
    ]
    d_own = keep(columns(d, y * (2 * GROUP * DH), 2 * GROUP * DH), d_rows.at[y], local.at[3])
    for n in range(1, NZ):
        zs[2][n] = across(2, n)

    def text_of(b):
        return x * (NZ * NC) + b * NC + c

    for b in range(NZ):
        t = text_of(b)
        count = counts[t]
        live = [jnp.where(j < count, lists[j, t], -1) for j in range(MAXB)]

        def find(pos, _):
            p = ((pos // NZ) % NX) * (NZ * NC) + (pos % NZ) * NC + pos // (NX * NZ)
            at = jnp.int32(MAXB)
            for j in range(MAXB):
                at = jnp.where(live[j] == p, j, at)
            where[b, pos] = at
            return 0

        lax.fori_loop(0, NPOS, find, 0)
        weights[b, MAXB] = jnp.zeros((BLK, BLK), BF16)
        dscores[b, MAXB] = jnp.zeros((BLK, BLK), BF16)

    own_block(0, 1)
    pass_on(0, 0)
    own_block(0, 2)
    pass_on(0, 1)
    own_block(0, 3)
    own[0].wait()
    sib[0].append(over(0, 0, x))
    pass_on(0, 2)
    own_block(1, 1)
    pass_on(0, 3)
    sib[0].append(over(0, 1, left))
    pass_on(1, 0)
    own_block(1, 2)
    d_own.wait()
    for copy in ys:
        copy.wait_recv()
    ds = []
    for flip in range(2):
        group = h if flip == 0 else 1 - h
        for n in range(NZ):
            part = d_rows.at[:, :, pl.ds(pl.multiple_of((group * GROUP + z_of[n]) * DH, DH), DH)]
            dst = dh.at[z, :, h]
            if flip == 0 and n == 0:
                d_keep = keep(part, dst, local.at[4])
            else:
                m = flip * NZ + n
                ds.append(go(part, dst, d_send.at[m], d_recv.at[m], z_id(n, flip)))
    own_block(1, 3)
    own[1].wait()
    sib[1].append(over(1, 0, x))
    pass_on(1, 1)
    rest(0)
    own[2].wait()
    for copy in zs[2][1:] + sib[0]:
        copy.wait_recv()

    def listed(ref, b, out):
        t = text_of(b)
        for j in range(MAXB):
            p = lists[j, t]
            out[pl.ds(j * BLK, BLK), :] = ref[slot_of(p // (NZ * NC), (p // NC) % NZ, p % NC)]

    def softmax(b):
        listed(kh, b, k_rows.at[b])
        scores = lax.dot_general(k_rows[b], qh[b], LAST, preferred_element_type=F32)
        row = lax.broadcasted_iota(jnp.int32, scores.shape, 0)
        scores = jnp.where(row < counts[text_of(b)] * BLK, scores, -jnp.inf)
        top = jnp.max(scores, axis=0, keepdims=True)
        e = jnp.exp2((scores - top) * (SCALE * LOG2E))
        p = e * (1.0 / jnp.sum(e, axis=0, keepdims=True))
        probs[b] = p
        weights[b, :MAXB] = p.astype(BF16).reshape(MAXB, BLK, BLK)

    softmax(0)
    pass_on(1, 2)
    softmax(1)
    pass_on(1, 3)
    sib[1].append(over(1, 1, right))
    softmax(2)
    rest(1)
    softmax(3)
    d_keep.wait()
    for copy in sib[1] + ds:
        copy.wait_recv()

    parts = []

    def spread(m, src, out):
        for n in range(1, NZ):
            parts.append(go(
                src.at[z_of[n]], columns(out, z * DH, DH), oz_send.at[m, n], oz_recv.at[m, n],
                ctx_id(x, z_of[n], c),
            ))
        return keep(src.at[z], columns(out, z * DH, DH), local.at[5 + m])

    def backward(b, _):
        db = dh[b].astype(F32).reshape(BLK, DH).astype(BF16)
        d_cat[b] = db
        listed(vh, b, v_rows)
        vals = v_rows[...]
        w = weights[b, :MAXB].reshape(MAXB * BLK, BLK)
        dprobs = lax.dot_general(vals, db, LAST, preferred_element_type=F32)
        delta = jnp.sum(w.astype(F32) * dprobs, axis=0, keepdims=True)
        s = (probs[b] * (dprobs - delta)).astype(BF16)
        dscores[b, :MAXB] = s.reshape(MAXB, BLK, BLK)
        own_out[0, b] = lax.dot_general(w, vals, FIRST, preferred_element_type=F32).astype(BF16)
        own_out[1, b] = (
            lax.dot_general(s, k_rows[b], FIRST, preferred_element_type=F32) * SCALE
        ).astype(BF16)
        return 0

    lax.fori_loop(0, NZ, backward, 0)
    keeps = [spread(0, own_out.at[0], attn), spread(1, own_out.at[1], grad_q)]

    def group_grad(i, core, chip):
        tiles, rows = ((dscores, qh), (weights, d_cat))[i]
        base = core * (NX * NZ) + chip * NZ
        for s in range(NZ):
            for b in range(NZ):
                lhs[i, pl.ds(s * BLK, BLK), pl.ds(b * BLK, BLK)] = tiles[b, where[b, base + s]]
        total = jnp.dot(
            lhs[i], rows[...].reshape(NZ * BLK, DH), preferred_element_type=F32
        )
        if i == 0:
            total = total * SCALE
        return total.reshape(NZ, BLK, DH)

    order = ((far, left, right, x), (far, right, left, x))
    ahead, back = (to_right, to_left), (to_left, to_right)
    sent = [[None] * NX, [None] * NX]
    moves = [[], []]

    def ship(i, n, device):
        moves[i].append(go(
            sums.at[i, n], x_in.at[i, n], ox_send.at[i, n], ox_recv.at[i, n], device
        ))

    for n in range(NX):
        for i in range(2):
            give[i, n] = group_grad(i, 1 - c, order[i][n]).astype(BF16)
            sent[i][n] = go(
                give.at[i, n], sib_in.at[i, n], oc_send.at[i, n], oc_recv.at[i, n], sibling
            )
        for i in range(2):
            total = group_grad(i, c, order[i][n])
            sent[i][n].wait_recv()
            total = total + sib_in[i, n].astype(F32)
            if n == 2:
                moves[i][0].wait_recv()
                total = total + x_in[i, 0].astype(F32)
            if n == 3:
                moves[i][1].wait_recv()
                total = total + x_in[i, 1].astype(F32)
                moves[i][2].wait_recv()
                total = total + x_in[i, 2].astype(F32)
                final[i] = total.astype(BF16)
                keeps.append(spread(2 + i, final.at[i], (grad_k, grad_v)[i]))
            else:
                sums[i, n] = total.astype(BF16)
                ship(i, n, back[i] if n == 1 else ahead[i])
    for copy in parts:
        copy.wait_recv()
    for copy in keeps:
        copy.wait()
    for copy in copies:
        copy.wait_send()


def shards(queries, keys, values, d_out, block_lists, list_counts):
    hbm = pl.BlockSpec(memory_space=pl.ANY)
    smem = pl.BlockSpec(memory_space=pltpu.SMEM)
    dma = pltpu.SemaphoreType.DMA
    rows = BLK // (2 * NY)

    def vm(*shape, dtype=BF16):
        return pltpu.VMEM(shape, dtype)

    return pl.pallas_call(
        kernel,
        out_shape=(jax.ShapeDtypeStruct((BLK, GROUP * DH), BF16),) * 4,
        in_specs=[smem] * 2 + [hbm] * 4,
        out_specs=[hbm] * 4,
        scratch_shapes=[
            vm(NPOS, BLK, DH), vm(NPOS, BLK, DH), vm(NZ, BLK, DH), vm(NZ, NY, 2, rows, DH),
            vm(NY, rows, 2 * GROUP * DH), pltpu.SMEM((NZ, NPOS), jnp.int32),
            vm(NZ, MAXB * BLK, DH), vm(MAXB * BLK, DH), vm(NZ, MAXB * BLK, BLK, dtype=F32),
            vm(NZ, MAXB + 1, BLK, BLK), vm(NZ, MAXB + 1, BLK, BLK), vm(NZ, BLK, DH),
            vm(2, NZ, BLK, DH), vm(2, NZ * BLK, NZ * BLK), vm(2, NX, NZ, BLK, DH),
            vm(2, NX, NZ, BLK, DH), vm(2, 3, NZ, BLK, DH), vm(2, 3, NZ, BLK, DH),
            vm(2, NZ, BLK, DH),
            dma((3, NZ)), dma((3, NZ)), dma((2, 3, NZ)), dma((2, 3, NZ)), dma((2, NX)),
            dma((2, NX)), dma((NY,)), dma((NY,)), dma((2 * NZ,)), dma((2 * NZ,)),
            dma((4, NZ)), dma((4, NZ)), dma((2, 3)), dma((2, 3)), dma((2, NX)), dma((2, NX)),
            dma((9,)),
        ],
        compiler_params=pltpu.CompilerParams(
            collective_id=0, has_side_effects=True, vmem_limit_bytes=60 << 20
        ),
        name="attend",
    )(block_lists.T, list_counts, queries, keys, values, d_out)


def solution(mesh):
    spec = P("ctx", "head")
    return jax.shard_map(
        shards,
        mesh=mesh,
        in_specs=(spec, spec, spec, P(("ctx", "head"), None), P(), P()),
        out_specs=(spec,) * 4,
        check_vma=False,
    )
```

```python
import math

import jax
import jax.numpy as jnp
from jax import lax
from jax.experimental import pallas as pl
from jax.experimental.pallas import tpu as pltpu
from jax.sharding import PartitionSpec as P

DH = 128
BLK = 128
MAXB = 8
NX, NY, NZ, NC = 4, 8, 4, 2
NPOS = NX * NZ * NC
GROUP = 4
MESH = pl.DeviceIdType.MESH
BF16, F32 = jnp.bfloat16, jnp.float32
SCALE = 1.0 / math.sqrt(DH)
LOG2E = math.log2(math.e)
LAST = (((1,), (1,)), ((), ()))
FIRST = (((0,), (0,)), ((), ()))


def coords():
    i = lax.axis_index("ctx")
    return i // (NZ * NC), (i // NC) % NZ, i % NC


def head_coords():
    g = lax.axis_index("head")
    return g // 2, g % 2


def z_order(z):
    return [z, z + 1 - 2 * (z % 2), (z + 2) % NZ, NZ - 1 - z]


def ctx_id(x, z, c):
    return {"ctx": x * (NZ * NC) + z * NC + c}


def slot_of(x, z, c):
    return c * (NX * NZ) + x * NZ + z


def send(src, dst, send_sem, recv_sem, device):
    copy = pltpu.make_async_remote_copy(
        src_ref=src, dst_ref=dst, send_sem=send_sem, recv_sem=recv_sem,
        device_id=device, device_id_type=MESH,
    )
    copy.start()
    return copy


def columns(ref, start, width):
    return ref.at[:, pl.ds(pl.multiple_of(start, DH), width)]


def kernel(
    lists, counts, q, k, v, d, attn, grad_q, grad_k, grad_v,
    kh, vh, qh, dh, d_rows, where, k_rows, v_rows, probs, weights, dscores, d_cat, own_out,
    lhs, give, sib_in, sums, x_in, final, stage, d_stage,
    z_send, z_recv, x_send, x_recv, c_send, c_recv, y_send, y_recv, d_send, d_recv,
    oz_send, oz_recv, ox_send, ox_recv, oc_send, oc_recv, local, stage_sem, d_sem,
):
    x, z, c = coords()
    y, h = head_coords()
    right, left, far = (x + 1) % NX, (x + 3) % NX, (x + 2) % NX
    to_right, to_left, sibling = ctx_id(right, z, c), ctx_id(left, z, c), ctx_id(x, z, 1 - c)
    z_of = z_order(z)

    def z_id(n, flip):
        return {**ctx_id(x, z_of[n], c), "head": 2 * y + (h if flip == 0 else 1 - h)}

    def y_id(r):
        return {"head": 2 * ((y + r) % NY) + h}

    partners = (
        [ctx_id(x, z_of[n], c) for n in range(1, NZ)]
        + [to_right, to_left, sibling]
        + [y_id(r) for r in range(1, NY)]
        + [z_id(n, 1) for n in range(NZ)]
    )
    barrier = pltpu.get_barrier_semaphore()
    for partner in partners:
        pl.semaphore_signal(barrier, inc=1, device_id=partner, device_id_type=MESH)
    copies = []

    def go(*args):
        copies.append(send(*args))
        return copies[-1]

    def keep(src, dst, sem):
        copy = pltpu.make_async_copy(src, dst, sem)
        copy.start()
        return copy

    ins, outs = (k, v, q), (kh, vh, qh)
    places = (slot_of(x, z, c), slot_of(x, z, c), z)
    own = [
        keep(columns(ins[i], z * DH, DH), outs[i].at[places[i]], local.at[i]) for i in range(3)
    ]
    staging = [
        [
            keep(columns(ins[i], z_of[n] * DH, DH), stage.at[i, n - 1], stage_sem.at[i, n - 1])
            for n in range(1, NZ)
        ]
        for i in range(3)
    ]
    d_stages = [
        keep(
            columns(d, ((y + r) % NY) * (2 * GROUP * DH), 2 * GROUP * DH),
            d_rows.at[y] if r == 0 else d_stage.at[r - 1], d_sem.at[r],
        )
        for r in range(NY)
    ]

    def text_of(b):
        return x * (NZ * NC) + b * NC + c

    for b in range(NZ):
        t = text_of(b)
        count = counts[t]
        live = [jnp.where(j < count, lists[j, t], -1) for j in range(MAXB)]

        def find(pos, _):
            p = ((pos // NZ) % NX) * (NZ * NC) + (pos % NZ) * NC + pos // (NX * NZ)
            at = jnp.int32(MAXB)
            for j in range(MAXB):
                at = jnp.where(live[j] == p, j, at)
            where[b, pos] = at
            return 0

        lax.fori_loop(0, NPOS, find, 0)
        weights[b, MAXB] = jnp.zeros((BLK, BLK), BF16)
        dscores[b, MAXB] = jnp.zeros((BLK, BLK), BF16)

    pl.semaphore_wait(barrier, len(partners))

    def across(i, n):
        staging[i][n - 1].wait()
        return go(
            stage.at[i, n - 1], outs[i].at[places[i]],
            z_send.at[i, n], z_recv.at[i, n], ctx_id(x, z_of[n], c),
        )

    def along(i, n, role):
        to = (to_right, to_left, (to_right, to_left)[i])[role]
        chip = (x, x, (left, right)[i])[role]
        dst = outs[i].at[slot_of(chip, z_of[n], c)]
        return go(dst, dst, x_send.at[i, role, n], x_recv.at[i, role, n], to)

    def over(i, m, chip):
        part = outs[i].at[pl.ds(c * (NX * NZ) + chip * NZ, NZ)]
        return go(part, part, c_send.at[i, m], c_recv.at[i, m], sibling)

    zs = [[None] * NZ for _ in range(3)]
    xs = [[[None] * NZ for _ in range(3)] for _ in range(2)]
    sib = [[], []]

    def own_block(i, n):
        if n > 0:
            zs[i][n].wait_recv()
        for role in range(2):
            xs[i][role][n] = along(i, n, role)

    def pass_on(i, n):
        xs[i][i][n].wait_recv()
        xs[i][2][n] = along(i, n, 2)

    def rest(i):
        other = 1 - i
        for n in range(NZ):
            xs[i][other][n].wait_recv()
        sib[i].append(over(i, 2, (right, left)[i]))
        for n in range(NZ):
            xs[i][2][n].wait_recv()
        sib[i].append(over(i, 3, far))

    for n in range(1, NZ):
        for i in range(2):
            zs[i][n] = across(i, n)
    for i in range(2):
        own[i].wait()
        own_block(i, 0)
    for r in range(1, NY):
        d_stages[r].wait()
    ys = [
        go(
            d_stage.at[r - 1], d_rows.at[y],
            y_send.at[r], y_recv.at[r], y_id(r),
        )
        for r in range(1, NY)
    ]

    for n in range(1, NZ):
        for i in range(2):
            own_block(i, n)
        for i in range(2):
            pass_on(i, n - 1)
    for n in range(1, NZ):
        zs[2][n] = across(2, n)
    for i in range(2):
        sib[i].append(over(i, 0, x))
    d_stages[0].wait()
    for copy in ys:
        copy.wait_recv()
    ds = []
    for flip in range(2):
        group = h if flip == 0 else 1 - h
        for n in range(NZ):
            part = d_rows.at[:, :, pl.ds(pl.multiple_of((group * GROUP + z_of[n]) * DH, DH), DH)]
            dst = dh.at[z, :, h]
            if flip == 0 and n == 0:
                d_keep = keep(part, dst, local.at[4])
            else:
                m = flip * NZ + n
                ds.append(go(part, dst, d_send.at[m], d_recv.at[m], z_id(n, flip)))
    for i in range(2):
        pass_on(i, NZ - 1)
        sib[i].append(over(i, 1, (left, right)[i]))
    rest(0)
    rest(1)
    own[2].wait()
    for copy in zs[2][1:] + sib[0]:
        copy.wait_recv()

    def listed(ref, b, out):
        t = text_of(b)
        for j in range(MAXB):
            p = lists[j, t]
            out[pl.ds(j * BLK, BLK), :] = ref[slot_of(p // (NZ * NC), (p // NC) % NZ, p % NC)]

    def softmax(b):
        listed(kh, b, k_rows.at[b])
        scores = lax.dot_general(k_rows[b], qh[b], LAST, preferred_element_type=F32)
        row = lax.broadcasted_iota(jnp.int32, scores.shape, 0)
        scores = jnp.where(row < counts[text_of(b)] * BLK, scores, -jnp.inf)
        top = jnp.max(scores, axis=0, keepdims=True)
        e = jnp.exp2((scores - top) * (SCALE * LOG2E))
        p = e * (1.0 / jnp.sum(e, axis=0, keepdims=True))
        probs[b] = p
        weights[b, :MAXB] = p.astype(BF16).reshape(MAXB, BLK, BLK)

    for b in range(NZ):
        softmax(b)
    d_keep.wait()
    for copy in sib[1] + ds:
        copy.wait_recv()

    parts = []

    def spread(m, src, out):
        for n in range(1, NZ):
            parts.append(go(
                src.at[z_of[n]], columns(out, z * DH, DH), oz_send.at[m, n], oz_recv.at[m, n],
                ctx_id(x, z_of[n], c),
            ))
        return keep(src.at[z], columns(out, z * DH, DH), local.at[5 + m])

    def backward(b, _):
        db = dh[b].astype(F32).reshape(BLK, DH).astype(BF16)
        d_cat[b] = db
        listed(vh, b, v_rows)
        vals = v_rows[...]
        w = weights[b, :MAXB].reshape(MAXB * BLK, BLK)
        dprobs = lax.dot_general(vals, db, LAST, preferred_element_type=F32)
        delta = jnp.sum(w.astype(F32) * dprobs, axis=0, keepdims=True)
        s = (probs[b] * (dprobs - delta)).astype(BF16)
        dscores[b, :MAXB] = s.reshape(MAXB, BLK, BLK)
        own_out[0, b] = lax.dot_general(w, vals, FIRST, preferred_element_type=F32).astype(BF16)
        own_out[1, b] = (
            lax.dot_general(s, k_rows[b], FIRST, preferred_element_type=F32) * SCALE
        ).astype(BF16)
        return 0

    lax.fori_loop(0, NZ, backward, 0)
    keeps = [spread(0, own_out.at[0], attn), spread(1, own_out.at[1], grad_q)]

    def group_grad(i, core, chip):
        tiles, rows = ((dscores, qh), (weights, d_cat))[i]
        base = core * (NX * NZ) + chip * NZ
        for s in range(NZ):
            for b in range(NZ):
                lhs[i, pl.ds(s * BLK, BLK), pl.ds(b * BLK, BLK)] = tiles[b, where[b, base + s]]
        total = jnp.dot(
            lhs[i], rows[...].reshape(NZ * BLK, DH), preferred_element_type=F32
        )
        if i == 0:
            total = total * SCALE
        return total.reshape(NZ, BLK, DH)

    order = ((far, left, right, x), (far, right, left, x))
    ahead, back = (to_right, to_left), (to_left, to_right)
    sent = [[None] * NX, [None] * NX]
    moves = [[], []]

    def ship(i, n, device):
        moves[i].append(go(
            sums.at[i, n], x_in.at[i, n], ox_send.at[i, n], ox_recv.at[i, n], device
        ))

    for n in range(NX):
        for i in range(2):
            give[i, n] = group_grad(i, 1 - c, order[i][n]).astype(BF16)
            sent[i][n] = go(
                give.at[i, n], sib_in.at[i, n], oc_send.at[i, n], oc_recv.at[i, n], sibling
            )
        for i in range(2):
            total = group_grad(i, c, order[i][n])
            sent[i][n].wait_recv()
            total = total + sib_in[i, n].astype(F32)
            if n == 2:
                moves[i][0].wait_recv()
                total = total + x_in[i, 0].astype(F32)
            if n == 3:
                moves[i][1].wait_recv()
                total = total + x_in[i, 1].astype(F32)
                moves[i][2].wait_recv()
                total = total + x_in[i, 2].astype(F32)
                final[i] = total.astype(BF16)
                keeps.append(spread(2 + i, final.at[i], (grad_k, grad_v)[i]))
            else:
                sums[i, n] = total.astype(BF16)
                ship(i, n, back[i] if n == 1 else ahead[i])
    for copy in parts:
        copy.wait_recv()
    for copy in keeps:
        copy.wait()
    for copy in copies:
        copy.wait_send()


def hand_out(*refs):
    ins, outs, sems = refs[:4], refs[4:8], refs[8]
    copies = [pltpu.make_async_copy(ins[i], outs[i], sems.at[i]) for i in range(4)]
    for copy in copies:
        copy.start()
    for copy in copies:
        copy.wait()


def shards(queries, keys, values, d_out, block_lists, list_counts):
    hbm = pl.BlockSpec(memory_space=pl.ANY)
    smem = pl.BlockSpec(memory_space=pltpu.SMEM)
    dma = pltpu.SemaphoreType.DMA
    rows = BLK // (2 * NY)

    def vm(*shape, dtype=BF16):
        return pltpu.VMEM(shape, dtype)

    in_place = pl.pallas_call(
        kernel,
        out_shape=(jax.ShapeDtypeStruct((BLK, GROUP * DH), BF16),) * 4,
        in_specs=[smem] * 2 + [hbm] * 4,
        out_specs=[hbm] * 4,
        scratch_shapes=[
            vm(NPOS, BLK, DH), vm(NPOS, BLK, DH), vm(NZ, BLK, DH), vm(NZ, NY, 2, rows, DH),
            vm(NY, rows, 2 * GROUP * DH), pltpu.SMEM((NZ, NPOS), jnp.int32),
            vm(NZ, MAXB * BLK, DH), vm(MAXB * BLK, DH), vm(NZ, MAXB * BLK, BLK, dtype=F32),
            vm(NZ, MAXB + 1, BLK, BLK), vm(NZ, MAXB + 1, BLK, BLK), vm(NZ, BLK, DH),
            vm(2, NZ, BLK, DH), vm(2, NZ * BLK, NZ * BLK), vm(2, NX, NZ, BLK, DH),
            vm(2, NX, NZ, BLK, DH), vm(2, 3, NZ, BLK, DH), vm(2, 3, NZ, BLK, DH),
            vm(2, NZ, BLK, DH), vm(3, NZ - 1, BLK, DH), vm(NY - 1, rows, 2 * GROUP * DH),
            dma((3, NZ)), dma((3, NZ)), dma((2, 3, NZ)), dma((2, 3, NZ)), dma((2, NX)),
            dma((2, NX)), dma((NY,)), dma((NY,)), dma((2 * NZ,)), dma((2 * NZ,)),
            dma((4, NZ)), dma((4, NZ)), dma((2, 3)), dma((2, 3)), dma((2, NX)), dma((2, NX)),
            dma((9,)), dma((3, NZ - 1)), dma((NY,)),
        ],
        compiler_params=pltpu.CompilerParams(
            collective_id=0, has_side_effects=True, vmem_limit_bytes=40 << 20
        ),
        name="attend",
    )(*(
        pltpu.with_memory_space_constraint(a, pltpu.HBM)
        for a in (block_lists.T, list_counts, queries, keys, values, d_out)
    ))
    return pl.pallas_call(
        hand_out,
        out_shape=(jax.ShapeDtypeStruct((BLK, GROUP * DH), BF16),) * 4,
        in_specs=[pl.BlockSpec(memory_space=pltpu.VMEM)] * 4,
        out_specs=[hbm] * 4,
        scratch_shapes=[dma((4,))],
        name="hand_out",
    )(*(pltpu.with_memory_space_constraint(a, pltpu.VMEM) for a in in_place))


def solution(mesh):
    spec = P("ctx", "head")
    return jax.shard_map(
        shards,
        mesh=mesh,
        in_specs=(spec, spec, spec, P(("ctx", "head"), None), P(), P()),
        out_specs=(spec,) * 4,
        check_vma=False,
    )
```

```python
import math

import jax
import jax.numpy as jnp
from jax import lax
from jax.experimental import pallas as pl
from jax.experimental.pallas import tpu as pltpu
from jax.sharding import PartitionSpec as P

DH = 128
BLK = 128
MAXB = 8
NX, NY, NZ, NC = 4, 8, 4, 2
NPOS = NX * NZ * NC
GROUP = 4
MESH = pl.DeviceIdType.MESH
BF16, F32 = jnp.bfloat16, jnp.float32
SCALE = 1.0 / math.sqrt(DH)
LOG2E = math.log2(math.e)
LAST = (((1,), (1,)), ((), ()))
FIRST = (((0,), (0,)), ((), ()))


def coords():
    i = lax.axis_index("ctx")
    return i // (NZ * NC), (i // NC) % NZ, i % NC


def head_coords():
    g = lax.axis_index("head")
    return g // 2, g % 2


def z_order(z):
    return [z, z + 1 - 2 * (z % 2), (z + 2) % NZ, NZ - 1 - z]


def ctx_id(x, z, c):
    return {"ctx": x * (NZ * NC) + z * NC + c}


def slot_of(x, z, c):
    return c * (NX * NZ) + x * NZ + z


def send(src, dst, send_sem, recv_sem, device):
    copy = pltpu.make_async_remote_copy(
        src_ref=src, dst_ref=dst, send_sem=send_sem, recv_sem=recv_sem,
        device_id=device, device_id_type=MESH,
    )
    copy.start()
    return copy


def columns(ref, start, width):
    return ref.at[:, pl.ds(pl.multiple_of(start, DH), width)]


def kernel(
    lists, counts, q, k, v, d, attn, grad_q, grad_k, grad_v,
    kh, vh, qh, dh, d_rows, where, k_rows, v_rows, probs, weights, shares, d_cat, own_out,
    give, sib_in, sums, x_in, final, stage, d_stage,
    z_send, z_recv, x_send, x_recv, c_send, c_recv, y_send, y_recv, d_send, d_recv,
    oz_send, oz_recv, ox_send, ox_recv, oc_send, oc_recv, local, stage_sem, d_sem,
):
    x, z, c = coords()
    y, h = head_coords()
    right, left, far = (x + 1) % NX, (x + 3) % NX, (x + 2) % NX
    to_right, to_left, sibling = ctx_id(right, z, c), ctx_id(left, z, c), ctx_id(x, z, 1 - c)
    to_far = ctx_id(far, z, c)
    z_of = z_order(z)

    def z_id(n, flip):
        return {**ctx_id(x, z_of[n], c), "head": 2 * y + (h if flip == 0 else 1 - h)}

    def y_id(r):
        return {"head": 2 * ((y + r) % NY) + h}

    partners = (
        [ctx_id(x, z_of[n], c) for n in range(1, NZ)]
        + [to_right, to_left, to_far, sibling]
        + [y_id(r) for r in range(1, NY)]
        + [z_id(n, 1) for n in range(NZ)]
    )
    barrier = pltpu.get_barrier_semaphore()
    for partner in partners:
        pl.semaphore_signal(barrier, inc=1, device_id=partner, device_id_type=MESH)
    copies = []

    def go(*args):
        copies.append(send(*args))
        return copies[-1]

    def keep(src, dst, sem):
        copy = pltpu.make_async_copy(src, dst, sem)
        copy.start()
        return copy

    ins, outs = (k, v, q), (kh, vh, qh)
    places = (slot_of(x, z, c), slot_of(x, z, c), z)
    own = [
        keep(columns(ins[i], z * DH, DH), outs[i].at[places[i]], local.at[i]) for i in range(3)
    ]
    staging = [
        [
            keep(columns(ins[i], z_of[n] * DH, DH), stage.at[i, n - 1], stage_sem.at[i, n - 1])
            for n in range(1, NZ)
        ]
        for i in range(3)
    ]
    d_stages = [
        keep(
            columns(d, ((y + r) % NY) * (2 * GROUP * DH), 2 * GROUP * DH),
            d_rows.at[y] if r == 0 else d_stage.at[r - 1], d_sem.at[r],
        )
        for r in range(NY)
    ]

    def text_of(b):
        return x * (NZ * NC) + b * NC + c

    for b in range(NZ):
        t = text_of(b)
        count = counts[t]
        live = [jnp.where(j < count, lists[j, t], -1) for j in range(MAXB)]

        def find(pos, _):
            p = ((pos // NZ) % NX) * (NZ * NC) + (pos % NZ) * NC + pos // (NX * NZ)
            at = jnp.int32(MAXB)
            for j in range(MAXB):
                at = jnp.where(live[j] == p, j, at)
            where[b, pos] = at
            return 0

        lax.fori_loop(0, NPOS, find, 0)
        for i in range(2):
            shares[i, b, MAXB] = jnp.zeros((BLK, DH), F32)

    pl.semaphore_wait(barrier, len(partners))

    def across(i, n):
        staging[i][n - 1].wait()
        return go(
            stage.at[i, n - 1], outs[i].at[places[i]],
            z_send.at[i, n], z_recv.at[i, n], ctx_id(x, z_of[n], c),
        )

    def along(i, n, role):
        passed = i == 1 and role == 2
        chip = (left, right)[n // 2] if passed else x
        to = (to_right, to_left)[n // 2] if passed else (to_right, to_left, to_far)[role]
        part = outs[i].at[slot_of(chip, z_of[n], c)]
        return go(part, part, x_send.at[i, role, n], x_recv.at[i, role, n], to)

    def over(i, m, chip):
        part = outs[i].at[pl.ds(c * (NX * NZ) + chip * NZ, NZ)]
        return go(part, part, c_send.at[i, m], c_recv.at[i, m], sibling)

    zs = [[None] * NZ for _ in range(3)]
    xs = [[[None] * NZ for _ in range(3)] for _ in range(2)]
    sib = [[], []]

    def own_block(i, n):
        if n > 0:
            zs[i][n].wait_recv()
        for role in (2, 0, 1) if i == 0 else (0, 1):
            xs[i][role][n] = along(i, n, role)

    def pass_on(n):
        xs[1][n // 2][n].wait_recv()
        xs[1][2][n] = along(1, n, 2)

    def share(i, m):
        for n in range(NZ):
            if m > 0 and not (i == 1 and m - 1 == n // 2):
                xs[i][m - 1][n].wait_recv()
        sib[i].append(over(i, m, (x, left, right, far)[m]))

    for n in range(1, NZ):
        zs[0][n] = across(0, n)
    own[0].wait()
    own_block(0, 0)
    ys = []
    for r in range(1, NY):
        d_stages[r].wait()
        ys.append(go(d_stage.at[r - 1], d_rows.at[y], y_send.at[r], y_recv.at[r], y_id(r)))
    for n in range(1, NZ):
        zs[2][n] = across(2, n)
    own_block(0, 1)
    own[1].wait()
    own_block(1, 0)
    for n in range(1, NZ):
        zs[1][n] = across(1, n)
    own_block(0, 2)
    own_block(0, 3)
    share(0, 0)
    d_stages[0].wait()
    for copy in ys:
        copy.wait_recv()
    ds = []
    for flip in range(2):
        group = h if flip == 0 else 1 - h
        for n in range(NZ):
            part = d_rows.at[:, :, pl.ds(pl.multiple_of((group * GROUP + z_of[n]) * DH, DH), DH)]
            dst = dh.at[z, :, h]
            if flip == 0 and n == 0:
                d_keep = keep(part, dst, local.at[4])
            else:
                m = flip * NZ + n
                ds.append(go(part, dst, d_send.at[m], d_recv.at[m], z_id(n, flip)))
    pass_on(0)
    own_block(1, 1)
    share(0, 1)
    share(0, 2)
    own_block(1, 2)
    own_block(1, 3)
    share(1, 0)
    share(0, 3)
    pass_on(1)
    own[2].wait()
    for copy in zs[2][1:] + sib[0]:
        copy.wait_recv()

    def listed(ref, b, out):
        t = text_of(b)
        for j in range(MAXB):
            p = lists[j, t]
            out[pl.ds(j * BLK, BLK), :] = ref[slot_of(p // (NZ * NC), (p // NC) % NZ, p % NC)]

    def softmax(b):
        listed(kh, b, k_rows.at[b])
        scores = lax.dot_general(k_rows[b], qh[b], LAST, preferred_element_type=F32)
        row = lax.broadcasted_iota(jnp.int32, scores.shape, 0)
        scores = jnp.where(row < counts[text_of(b)] * BLK, scores, -jnp.inf)
        top = jnp.max(scores, axis=0, keepdims=True)
        e = jnp.exp2((scores - top) * (SCALE * LOG2E))
        p = e * (1.0 / jnp.sum(e, axis=0, keepdims=True))
        probs[b] = p
        weights[b] = p.astype(BF16).reshape(MAXB, BLK, BLK)

    softmax(0)
    pass_on(2)
    pass_on(3)
    softmax(1)
    share(1, 1)
    share(1, 2)
    softmax(2)
    softmax(3)
    d_keep.wait()
    for copy in ds:
        copy.wait_recv()
    for b in range(NZ):
        d_cat[b] = dh[b].astype(F32).reshape(BLK, DH).astype(BF16)

    parts = []

    def spread(m, src, out):
        for n in range(1, NZ):
            parts.append(go(
                src.at[z_of[n]], columns(out, z * DH, DH), oz_send.at[m, n], oz_recv.at[m, n],
                ctx_id(x, z_of[n], c),
            ))
        parts_own.append(keep(src.at[z], columns(out, z * DH, DH), local.at[5 + m]))

    parts_own = []

    def backward(b):
        db = d_cat[b]
        listed(vh, b, v_rows)
        vals = v_rows[...]
        w = weights[b].reshape(MAXB * BLK, BLK)
        dprobs = lax.dot_general(vals, db, LAST, preferred_element_type=F32)
        delta = jnp.sum(w.astype(F32) * dprobs, axis=0, keepdims=True)
        s = (probs[b] * (dprobs - delta)).astype(BF16)
        shares[0, b, :MAXB] = (
            jnp.dot(s, qh[b], preferred_element_type=F32) * SCALE
        ).reshape(MAXB, BLK, DH)
        own_out[0, b] = lax.dot_general(w, vals, FIRST, preferred_element_type=F32).astype(BF16)
        own_out[1, b] = (
            lax.dot_general(s, k_rows[b], FIRST, preferred_element_type=F32) * SCALE
        ).astype(BF16)

    def block_grad(i, core, chip, s):
        p = slot_of(chip, s, core)
        total = shares[i, 0, where[0, p]]
        for b in range(1, NZ):
            total = total + shares[i, b, where[b, p]]
        return total

    chips = (far, left, right, x)
    halves = (range(NZ // 2), range(NZ // 2, NZ))
    given = [[None] * NX, [None] * NX]
    moves = [{}, {}]

    def give_sibling(i, n):
        for s in range(NZ):
            give[i, n, s] = block_grad(i, 1 - c, chips[n], s).astype(BF16)
        given[i][n] = go(
            give.at[i, n], sib_in.at[i, n], oc_send.at[i, n], oc_recv.at[i, n], sibling
        )

    def core_sum(i, n, s):
        return block_grad(i, c, chips[n], s) + sib_in[i, n, s].astype(F32)

    def ship(i, role, half, blocks, device):
        for s in range(NZ // 2):
            sums[i, role, half, s] = blocks(halves[half][s]).astype(BF16)
        moves[i][role, half] = go(
            sums.at[i, role, half], x_in.at[i, role, half],
            ox_send.at[i, role, half], ox_recv.at[i, role, half], device,
        )

    def first_steps(i):
        for n in range(NX):
            give_sibling(i, n)
        for n, role in ((0, 0), (2, 1), (1, 1)):
            given[i][n].wait_recv()
            for half, device in ((0, to_right), (1, to_left)):
                if i == 0:
                    ship(i, n, half, lambda s: core_sum(i, n, s), (to_far, to_left, to_right)[n])
                elif role == 0:
                    ship(i, 0, half, lambda s: core_sum(i, 0, s), device)
                elif (n == 1) == (half == 0):
                    ship(i, 1, half, lambda s: core_sum(i, n, s), to_left if n == 1 else to_right)

    def middle_steps(i):
        for half, n, device in ((0, 2, to_right), (1, 1, to_left)):
            moves[i][0, half].wait_recv()
            ship(
                i, 2, half,
                lambda s: core_sum(i, n, s) + x_in[i, 0, half, s % (NZ // 2)].astype(F32), device,
            )

    def last_steps(i):
        given[i][3].wait_recv()
        for role in range(3) if i == 0 else (1, 2):
            for half in range(2):
                moves[i][role, half].wait_recv()
        out = (grad_k, grad_v)[i]
        for n in range(NZ - 1, -1, -1):
            s = z_of[n]
            half, at = s // (NZ // 2), s % (NZ // 2)
            total = core_sum(i, 3, s)
            for role in range(3) if i == 0 else (1, 2):
                total = total + x_in[i, role, half, at].astype(F32)
            final[i, s] = total.astype(BF16)
            if n == 0:
                parts_own.append(keep(final.at[i, z], columns(out, z * DH, DH), local.at[7 + i]))
            else:
                parts.append(go(
                    final.at[i, s], columns(out, z * DH, DH), oz_send.at[2 + i, n],
                    oz_recv.at[2 + i, n], ctx_id(x, s, c),
                ))

    for b in range(NZ):
        shares[1, b, :MAXB] = jnp.dot(
            weights[b].reshape(MAXB * BLK, BLK), d_cat[b], preferred_element_type=F32
        ).reshape(MAXB, BLK, DH)
    first_steps(1)
    share(1, 3)
    for copy in sib[1]:
        copy.wait_recv()
    backward(0)
    middle_steps(1)
    backward(1)
    backward(2)
    backward(3)
    spread(0, own_out.at[0], attn)
    spread(1, own_out.at[1], grad_q)
    first_steps(0)
    last_steps(1)
    last_steps(0)
    for copy in parts:
        copy.wait_recv()
    for copy in parts_own:
        copy.wait()
    for copy in copies:
        copy.wait_send()


def hand_out(*refs):
    ins, outs, sems = refs[:4], refs[4:8], refs[8]
    copies = [pltpu.make_async_copy(ins[i], outs[i], sems.at[i]) for i in range(4)]
    for copy in copies:
        copy.start()
    for copy in copies:
        copy.wait()


def shards(queries, keys, values, d_out, block_lists, list_counts):
    hbm = pl.BlockSpec(memory_space=pl.ANY)
    smem = pl.BlockSpec(memory_space=pltpu.SMEM)
    dma = pltpu.SemaphoreType.DMA
    rows = BLK // (2 * NY)

    def vm(*shape, dtype=BF16):
        return pltpu.VMEM(shape, dtype)

    in_place = pl.pallas_call(
        kernel,
        out_shape=(jax.ShapeDtypeStruct((BLK, GROUP * DH), BF16),) * 4,
        in_specs=[smem] * 2 + [hbm] * 4,
        out_specs=[hbm] * 4,
        scratch_shapes=[
            vm(NPOS, BLK, DH), vm(NPOS, BLK, DH), vm(NZ, BLK, DH), vm(NZ, NY, 2, rows, DH),
            vm(NY, rows, 2 * GROUP * DH), pltpu.SMEM((NZ, NPOS), jnp.int32),
            vm(NZ, MAXB * BLK, DH), vm(MAXB * BLK, DH), vm(NZ, MAXB * BLK, BLK, dtype=F32),
            vm(NZ, MAXB, BLK, BLK), vm(2, NZ, MAXB + 1, BLK, DH, dtype=F32), vm(NZ, BLK, DH),
            vm(2, NZ, BLK, DH), vm(2, NX, NZ, BLK, DH),
            vm(2, NX, NZ, BLK, DH), vm(2, 3, 2, NZ // 2, BLK, DH), vm(2, 3, 2, NZ // 2, BLK, DH),
            vm(2, NZ, BLK, DH), vm(3, NZ - 1, BLK, DH), vm(NY - 1, rows, 2 * GROUP * DH),
            dma((3, NZ)), dma((3, NZ)), dma((2, 3, NZ)), dma((2, 3, NZ)), dma((2, NX)),
            dma((2, NX)), dma((NY,)), dma((NY,)), dma((2 * NZ,)), dma((2 * NZ,)),
            dma((4, NZ)), dma((4, NZ)), dma((2, 3, 2)), dma((2, 3, 2)), dma((2, NX)), dma((2, NX)),
            dma((9,)), dma((3, NZ - 1)), dma((NY,)),
        ],
        compiler_params=pltpu.CompilerParams(
            collective_id=0, has_side_effects=True, vmem_limit_bytes=40 << 20
        ),
        name="attend",
    )(*(
        pltpu.with_memory_space_constraint(a, pltpu.HBM)
        for a in (block_lists.T, list_counts, queries, keys, values, d_out)
    ))
    return pl.pallas_call(
        hand_out,
        out_shape=(jax.ShapeDtypeStruct((BLK, GROUP * DH), BF16),) * 4,
        in_specs=[pl.BlockSpec(memory_space=pltpu.VMEM)] * 4,
        out_specs=[hbm] * 4,
        scratch_shapes=[dma((4,))],
        name="hand_out",
    )(*(pltpu.with_memory_space_constraint(a, pltpu.VMEM) for a in in_place))


def solution(mesh):
    spec = P("ctx", "head")
    return jax.shard_map(
        shards,
        mesh=mesh,
        in_specs=(spec, spec, spec, P(("ctx", "head"), None), P(), P()),
        out_specs=(spec,) * 4,
        check_vma=False,
    )
```

```python
import math

import jax
import jax.numpy as jnp
from jax import lax
from jax.experimental import pallas as pl
from jax.experimental.pallas import tpu as pltpu
from jax.sharding import PartitionSpec as P

DH = 128
BLK = 128
MAXB = 8
NX, NY, NZ, NC = 4, 8, 4, 2
NPOS = NX * NZ * NC
GROUP = 4
MESH = pl.DeviceIdType.MESH
BF16, F32 = jnp.bfloat16, jnp.float32
SCALE = 1.0 / math.sqrt(DH)
LOG2E = math.log2(math.e)
LAST = (((1,), (1,)), ((), ()))
FIRST = (((0,), (0,)), ((), ()))


def coords():
    i = lax.axis_index("ctx")
    return i // (NZ * NC), (i // NC) % NZ, i % NC


def head_coords():
    g = lax.axis_index("head")
    return g // 2, g % 2


def z_order(z):
    return [z, z + 1 - 2 * (z % 2), (z + 2) % NZ, NZ - 1 - z]


def ctx_id(x, z, c):
    return {"ctx": x * (NZ * NC) + z * NC + c}


def slot_of(x, z, c):
    return c * (NX * NZ) + x * NZ + z


def send(src, dst, send_sem, recv_sem, device):
    copy = pltpu.make_async_remote_copy(
        src_ref=src, dst_ref=dst, send_sem=send_sem, recv_sem=recv_sem,
        device_id=device, device_id_type=MESH,
    )
    copy.start()
    return copy


def columns(ref, start, width):
    return ref.at[:, pl.ds(pl.multiple_of(start, DH), width)]


def kernel(
    lists, counts, q, k, v, d, attn, grad_q, grad_k, grad_v,
    kh, vh, qh, dh, d_rows, where, k_rows, v_rows, probs, weights, shares, d_cat, own_out,
    give, sib_in, sums, x_in, final, stage, d_stage,
    z_send, z_recv, x_send, x_recv, c_send, c_recv, y_send, y_recv, d_send, d_recv,
    oz_send, oz_recv, ox_send, ox_recv, oc_send, oc_recv, local, stage_sem, d_sem,
):
    x, z, c = coords()
    y, h = head_coords()
    right, left, far = (x + 1) % NX, (x + 3) % NX, (x + 2) % NX
    to_right, to_left, sibling = ctx_id(right, z, c), ctx_id(left, z, c), ctx_id(x, z, 1 - c)
    to_far = ctx_id(far, z, c)
    z_of = z_order(z)

    def z_id(n, flip):
        return {**ctx_id(x, z_of[n], c), "head": 2 * y + (h if flip == 0 else 1 - h)}

    def y_id(r):
        return {"head": 2 * ((y + r) % NY) + h}

    partners = (
        [ctx_id(x, z_of[n], c) for n in range(1, NZ)]
        + [to_right, to_left, to_far, sibling]
        + [y_id(r) for r in range(1, NY)]
        + [z_id(n, 1) for n in range(NZ)]
    )
    barrier = pltpu.get_barrier_semaphore()
    for partner in partners:
        pl.semaphore_signal(barrier, inc=1, device_id=partner, device_id_type=MESH)
    copies = []

    def go(*args):
        copies.append(send(*args))
        return copies[-1]

    def keep(src, dst, sem):
        copy = pltpu.make_async_copy(src, dst, sem)
        copy.start()
        return copy

    ins, outs = (k, v, q), (kh, vh, qh)
    places = (slot_of(x, z, c), slot_of(x, z, c), z)
    own = [
        keep(columns(ins[i], z * DH, DH), outs[i].at[places[i]], local.at[i]) for i in range(3)
    ]
    staging = [
        [
            keep(columns(ins[i], z_of[n] * DH, DH), stage.at[i, n - 1], stage_sem.at[i, n - 1])
            for n in range(1, NZ)
        ]
        for i in range(3)
    ]
    d_stages = [
        keep(
            columns(d, ((y + r) % NY) * (2 * GROUP * DH), 2 * GROUP * DH),
            d_rows.at[y] if r == 0 else d_stage.at[r - 1], d_sem.at[r],
        )
        for r in range(NY)
    ]

    def text_of(b):
        return x * (NZ * NC) + b * NC + c

    for b in range(NZ):
        t = text_of(b)
        count = counts[t]
        live = [jnp.where(j < count, lists[j, t], -1) for j in range(MAXB)]

        def find(pos, _):
            p = ((pos // NZ) % NX) * (NZ * NC) + (pos % NZ) * NC + pos // (NX * NZ)
            at = jnp.int32(MAXB)
            for j in range(MAXB):
                at = jnp.where(live[j] == p, j, at)
            where[b, pos] = at
            return 0

        lax.fori_loop(0, NPOS, find, 0)
        for i in range(2):
            shares[i, b, MAXB] = jnp.zeros((BLK, DH), F32)

    pl.semaphore_wait(barrier, len(partners))

    def across(i, n):
        staging[i][n - 1].wait()
        return go(
            stage.at[i, n - 1], outs[i].at[places[i]],
            z_send.at[i, n], z_recv.at[i, n], ctx_id(x, z_of[n], c),
        )

    def along(i, n, role):
        passed = i == 1 and role == 2
        chip = (left, right)[n // 2] if passed else x
        to = (to_right, to_left)[n // 2] if passed else (to_right, to_left, to_far)[role]
        part = outs[i].at[slot_of(chip, z_of[n], c)]
        return go(part, part, x_send.at[i, role, n], x_recv.at[i, role, n], to)

    def over(i, m, chip):
        part = outs[i].at[pl.ds(c * (NX * NZ) + chip * NZ, NZ)]
        return go(part, part, c_send.at[i, m], c_recv.at[i, m], sibling)

    zs = [[None] * NZ for _ in range(3)]
    xs = [[[None] * NZ for _ in range(3)] for _ in range(2)]
    sib = [[], []]

    def own_block(i, n):
        if n > 0:
            zs[i][n].wait_recv()
        for role in (2, 0, 1) if i == 0 else (0, 1):
            xs[i][role][n] = along(i, n, role)

    def pass_on(n):
        xs[1][n // 2][n].wait_recv()
        xs[1][2][n] = along(1, n, 2)

    def share(i, m):
        for n in range(NZ):
            if m > 0 and not (i == 1 and m - 1 == n // 2):
                xs[i][m - 1][n].wait_recv()
        sib[i].append(over(i, m, (x, left, right, far)[m]))

    for n in range(1, NZ):
        zs[0][n] = across(0, n)
    own[0].wait()
    own_block(0, 0)
    ys = []
    for r in range(1, NY):
        d_stages[r].wait()
        ys.append(go(d_stage.at[r - 1], d_rows.at[y], y_send.at[r], y_recv.at[r], y_id(r)))
    for n in range(1, NZ):
        zs[2][n] = across(2, n)
    own_block(0, 1)
    own[1].wait()
    own_block(1, 0)
    for n in range(1, NZ):
        zs[1][n] = across(1, n)
    own_block(0, 2)
    own_block(0, 3)
    share(0, 0)
    d_stages[0].wait()
    for copy in ys:
        copy.wait_recv()
    ds = []
    for flip in range(2):
        group = h if flip == 0 else 1 - h
        for n in range(NZ):
            part = d_rows.at[:, :, pl.ds(pl.multiple_of((group * GROUP + z_of[n]) * DH, DH), DH)]
            dst = dh.at[z, :, h]
            if flip == 0 and n == 0:
                d_keep = keep(part, dst, local.at[4])
            else:
                m = flip * NZ + n
                ds.append(go(part, dst, d_send.at[m], d_recv.at[m], z_id(n, flip)))
    pass_on(0)
    own_block(1, 1)
    share(0, 1)
    share(0, 2)
    own_block(1, 2)
    own_block(1, 3)
    share(1, 0)
    share(0, 3)
    pass_on(1)
    own[2].wait()
    for copy in zs[2][1:] + sib[0]:
        copy.wait_recv()

    def listed(ref, b, out):
        t = text_of(b)
        for j in range(MAXB):
            p = lists[j, t]
            out[pl.ds(j * BLK, BLK), :] = ref[slot_of(p // (NZ * NC), (p // NC) % NZ, p % NC)]

    def softmax(b):
        listed(kh, b, k_rows.at[b])
        scores = lax.dot_general(k_rows[b], qh[b], LAST, preferred_element_type=F32)
        row = lax.broadcasted_iota(jnp.int32, scores.shape, 0)
        scores = jnp.where(row < counts[text_of(b)] * BLK, scores, -jnp.inf)
        top = jnp.max(scores, axis=0, keepdims=True)
        e = jnp.exp2((scores - top) * (SCALE * LOG2E))
        p = e * (1.0 / jnp.sum(e, axis=0, keepdims=True))
        probs[b] = p
        weights[b] = p.astype(BF16).reshape(MAXB, BLK, BLK)

    softmax(0)
    pass_on(2)
    pass_on(3)
    softmax(1)
    share(1, 1)
    share(1, 2)
    softmax(2)
    softmax(3)
    d_keep.wait()
    for copy in ds:
        copy.wait_recv()
    for b in range(NZ):
        d_cat[b] = dh[b].astype(F32).reshape(BLK, DH).astype(BF16)

    parts = []

    def spread(m, src, out):
        for n in range(1, NZ):
            parts.append(go(
                src.at[z_of[n]], columns(out, z * DH, DH), oz_send.at[m, n], oz_recv.at[m, n],
                ctx_id(x, z_of[n], c),
            ))
        parts_own.append(keep(src.at[z], columns(out, z * DH, DH), local.at[5 + m]))

    parts_own = []

    def backward(b):
        db = d_cat[b]
        listed(vh, b, v_rows)
        vals = v_rows[...]
        w = weights[b].reshape(MAXB * BLK, BLK)
        dprobs = lax.dot_general(vals, db, LAST, preferred_element_type=F32)
        delta = jnp.sum(w.astype(F32) * dprobs, axis=0, keepdims=True)
        s = (probs[b] * (dprobs - delta)).astype(BF16)
        shares[0, b, :MAXB] = (
            jnp.dot(s, qh[b], preferred_element_type=F32) * SCALE
        ).reshape(MAXB, BLK, DH)
        own_out[0, b] = lax.dot_general(w, vals, FIRST, preferred_element_type=F32).astype(BF16)
        own_out[1, b] = (
            lax.dot_general(s, k_rows[b], FIRST, preferred_element_type=F32) * SCALE
        ).astype(BF16)

    def block_grad(i, core, chip, s):
        p = slot_of(chip, s, core)
        total = shares[i, 0, where[0, p]]
        for b in range(1, NZ):
            total = total + shares[i, b, where[b, p]]
        return total

    chips = (far, left, right, x)
    halves = (range(NZ // 2), range(NZ // 2, NZ))
    given = [[None] * NX, [None] * NX]
    moves = [{}, {}]

    def give_sibling(i, n):
        for s in range(NZ):
            give[i, n, s] = block_grad(i, 1 - c, chips[n], s).astype(BF16)
        given[i][n] = go(
            give.at[i, n], sib_in.at[i, n], oc_send.at[i, n], oc_recv.at[i, n], sibling
        )

    def core_sum(i, n, s):
        return block_grad(i, c, chips[n], s) + sib_in[i, n, s].astype(F32)

    def ship(i, role, half, blocks, device):
        for s in range(NZ // 2):
            sums[i, role, half, s] = blocks(halves[half][s]).astype(BF16)
        moves[i][role, half] = go(
            sums.at[i, role, half], x_in.at[i, role, half],
            ox_send.at[i, role, half], ox_recv.at[i, role, half], device,
        )

    def give_steps(i):
        for n in range(NX):
            give_sibling(i, n)

    def first_steps(i):
        for n, role in ((0, 0), (2, 1), (1, 1)):
            given[i][n].wait_recv()
            for half, device in ((0, to_right), (1, to_left)):
                if i == 0:
                    ship(i, n, half, lambda s: core_sum(i, n, s), (to_far, to_left, to_right)[n])
                elif role == 0:
                    ship(i, 0, half, lambda s: core_sum(i, 0, s), device)
                elif (n == 1) == (half == 0):
                    ship(i, 1, half, lambda s: core_sum(i, n, s), to_left if n == 1 else to_right)

    def middle_steps(i):
        for half, n, device in ((0, 2, to_right), (1, 1, to_left)):
            moves[i][0, half].wait_recv()
            ship(
                i, 2, half,
                lambda s: core_sum(i, n, s) + x_in[i, 0, half, s % (NZ // 2)].astype(F32), device,
            )

    def last_steps(i):
        given[i][3].wait_recv()
        for role in range(3) if i == 0 else (1, 2):
            for half in range(2):
                moves[i][role, half].wait_recv()
        out = (grad_k, grad_v)[i]
        for n in range(NZ - 1, -1, -1):
            s = z_of[n]
            half, at = s // (NZ // 2), s % (NZ // 2)
            total = core_sum(i, 3, s)
            for role in range(3) if i == 0 else (1, 2):
                total = total + x_in[i, role, half, at].astype(F32)
            final[i, s] = total.astype(BF16)
            if n == 0:
                parts_own.append(keep(final.at[i, z], columns(out, z * DH, DH), local.at[7 + i]))
            else:
                parts.append(go(
                    final.at[i, s], columns(out, z * DH, DH), oz_send.at[2 + i, n],
                    oz_recv.at[2 + i, n], ctx_id(x, s, c),
                ))

    for b in range(NZ):
        shares[1, b, :MAXB] = jnp.dot(
            weights[b].reshape(MAXB * BLK, BLK), d_cat[b], preferred_element_type=F32
        ).reshape(MAXB, BLK, DH)
    give_steps(1)
    first_steps(1)
    share(1, 3)
    for copy in sib[1]:
        copy.wait_recv()
    backward(0)
    backward(1)
    backward(2)
    middle_steps(1)
    backward(3)
    early = len(copies)
    give_steps(0)
    spread(0, own_out.at[0], attn)
    spread(1, own_out.at[1], grad_q)
    first_steps(0)
    for copy in copies[:early]:
        copy.wait_send()
    last_steps(1)
    last_steps(0)
    for copy in parts:
        copy.wait_recv()
    for copy in parts_own:
        copy.wait()
    for copy in copies[early:]:
        copy.wait_send()


def hand_out(*refs):
    ins, outs, sems = refs[:4], refs[4:8], refs[8]
    copies = [pltpu.make_async_copy(ins[i], outs[i], sems.at[i]) for i in range(4)]
    for copy in copies:
        copy.start()
    for copy in copies:
        copy.wait()


def shards(queries, keys, values, d_out, block_lists, list_counts):
    hbm = pl.BlockSpec(memory_space=pl.ANY)
    smem = pl.BlockSpec(memory_space=pltpu.SMEM)
    dma = pltpu.SemaphoreType.DMA
    rows = BLK // (2 * NY)

    def vm(*shape, dtype=BF16):
        return pltpu.VMEM(shape, dtype)

    in_place = pl.pallas_call(
        kernel,
        out_shape=(jax.ShapeDtypeStruct((BLK, GROUP * DH), BF16),) * 4,
        in_specs=[smem] * 2 + [hbm] * 4,
        out_specs=[hbm] * 4,
        scratch_shapes=[
            vm(NPOS, BLK, DH), vm(NPOS, BLK, DH), vm(NZ, BLK, DH), vm(NZ, NY, 2, rows, DH),
            vm(NY, rows, 2 * GROUP * DH), pltpu.SMEM((NZ, NPOS), jnp.int32),
            vm(NZ, MAXB * BLK, DH), vm(MAXB * BLK, DH), vm(NZ, MAXB * BLK, BLK, dtype=F32),
            vm(NZ, MAXB, BLK, BLK), vm(2, NZ, MAXB + 1, BLK, DH, dtype=F32), vm(NZ, BLK, DH),
            vm(2, NZ, BLK, DH), vm(2, NX, NZ, BLK, DH),
            vm(2, NX, NZ, BLK, DH), vm(2, 3, 2, NZ // 2, BLK, DH), vm(2, 3, 2, NZ // 2, BLK, DH),
            vm(2, NZ, BLK, DH), vm(3, NZ - 1, BLK, DH), vm(NY - 1, rows, 2 * GROUP * DH),
            dma((3, NZ)), dma((3, NZ)), dma((2, 3, NZ)), dma((2, 3, NZ)), dma((2, NX)),
            dma((2, NX)), dma((NY,)), dma((NY,)), dma((2 * NZ,)), dma((2 * NZ,)),
            dma((4, NZ)), dma((4, NZ)), dma((2, 3, 2)), dma((2, 3, 2)), dma((2, NX)), dma((2, NX)),
            dma((9,)), dma((3, NZ - 1)), dma((NY,)),
        ],
        compiler_params=pltpu.CompilerParams(
            collective_id=0, has_side_effects=True, vmem_limit_bytes=40 << 20
        ),
        name="attend",
    )(*(
        pltpu.with_memory_space_constraint(a, pltpu.HBM)
        for a in (block_lists.T, list_counts, queries, keys, values, d_out)
    ))
    return pl.pallas_call(
        hand_out,
        out_shape=(jax.ShapeDtypeStruct((BLK, GROUP * DH), BF16),) * 4,
        in_specs=[pl.BlockSpec(memory_space=pltpu.VMEM)] * 4,
        out_specs=[hbm] * 4,
        scratch_shapes=[dma((4,))],
        name="hand_out",
    )(*(pltpu.with_memory_space_constraint(a, pltpu.VMEM) for a in in_place))


def solution(mesh):
    spec = P("ctx", "head")
    return jax.shard_map(
        shards,
        mesh=mesh,
        in_specs=(spec, spec, spec, P(("ctx", "head"), None), P(), P()),
        out_specs=(spec,) * 4,
        check_vma=False,
    )
```
